512 devices in a mesh: grid: 128 (over z, y, core), band: 4 (over x).
Axes of the slice: x: 4, y: 4, z: 16, core: 2. Of those that a mesh axis runs over, the one named last changes fastest.
Arguments:
- orbitals: bfloat16 [4096, 65536], P(('band', 'grid')), may hold values from -6 to 6
- w_first: bfloat16 [4096, 1024], P(('band', 'grid')), may hold values from -0.09375 to 0.09375
- w_second: bfloat16 [4096, 1024], P(('band', 'grid')), may hold values from -0.09375 to 0.09375
- pivots: int32 [128, 8, 256], P('grid'), may hold values from 0 to 511, as said below
Outputs:
- chosen: bfloat16 [1024, 256], replicated
- quality: float32 [128, 256], P('grid')
The draws below stay inside these ranges and needn't reach their ends.
Inputs may be any that keep to these rules, and one draw needn't show every extreme that they name: Each list pivots[g, r, :] holds distinct values below 512 and contains 2 * 256 - 1; indices g that agree in all bits from bit r upward have equal lists in round r.
All inputs are finite; a program needn't handle non-finite values.
Results may differ from the reference program's by a relative error of at most 0.0026.
Values may be sent and summed in bfloat16 or wider, within the bound.
A program may use at most 64 MiB of HBM per device.

```python
import jax
import jax.numpy as jnp

NB = 4096
SKETCH_WIDTH = 1024
C = 256
NG = 65536
ROUNDS = 8
N_GRID = 128


strengths = (0.9, 0.495, 0.272, 0.1497, 0.0823, 0.0453)


noise_level = 0.2


def draw_orbitals(key, part):
    key_rows, key_points, key_rough = jax.random.split(jax.random.fold_in(key, 4051), 3)
    profiles = len(strengths)
    row_factors = jax.random.normal(key_rows, (NB, profiles), jnp.float32)
    point_factors = jax.random.normal(key_points, (profiles, NG), jnp.float32)
    residue = jax.random.normal(key_rough, (NB, NG), jnp.float32)
    combined = noise_level * residue
    for profile in range(profiles):
        combined = combined + strengths[profile] * row_factors[:, profile:profile + 1] * point_factors[profile:profile + 1, :]
    return jnp.clip(combined, -6.0, 6.0).astype(jnp.bfloat16)


def draw_pivots(key, part):
    per_section = []
    for section in range(ROUNDS):

        def draw_list(group):
            subkey = jax.random.fold_in(jax.random.fold_in(key, 7919 + section), group)
            key_pick, key_order = jax.random.split(subkey)
            others = jax.random.permutation(key_pick, 2 * C - 1)[:C - 1].astype(jnp.int32)
            listed = jnp.concatenate([jnp.full((1,), 2 * C - 1, jnp.int32), others])
            return jax.random.permutation(key_order, listed)
        groups = jnp.arange(N_GRID, dtype=jnp.int32) >> section
        per_section.append(jax.vmap(draw_list)(groups))
    return jnp.stack(per_section, axis=1)


def block_levels(stream_key, extent, cuts, least, top_value):
    level = 1.0
    for position, shards_of in cuts:
        heights = jax.random.uniform(jax.random.fold_in(jax.random.fold_in(stream_key, 6), position), (shards_of,), jnp.float32, least / len(cuts), top_value / len(cuts))
        level = level * jnp.repeat(jnp.exp(heights), extent[position] // shards_of).reshape((-1,) + (1,) * (len(extent) - 1 - position))
    return level


def scatter_about(own_key, shape, deviation, bound, pieces=(), kind=jnp.bfloat16):
    entries = deviation * jax.random.normal(own_key, shape, jnp.float32)
    if pieces:
        entries = entries * block_levels(own_key, shape, pieces, -0.22, 0.18)
    return jnp.clip(entries, -bound, bound).astype(kind)


def setup_inputs(seed: int = 0) -> dict:
    splits = jax.random.split(jax.random.key(seed), 5)
    orbitals = draw_orbitals(jax.random.fold_in(splits[4], 71), 0)
    w_first = scatter_about(splits[1], (NB, SKETCH_WIDTH), NB ** -0.5, 0.09375, ((0, 512),))
    w_second = scatter_about(splits[2], (NB, SKETCH_WIDTH), NB ** -0.5, 0.09375, ((0, 512),))
    pivots = draw_pivots(jax.random.fold_in(splits[4], 71), 0)
    return {"orbitals": orbitals, "w_first": w_first, "w_second": w_second, "pivots": pivots}


ridge = 0.1

def log_pivots(chosen):
    widened_sketch = chosen.astype(jnp.float32)
    gram_product = jnp.einsum('vls,vli->vsi', widened_sketch, widened_sketch) / SKETCH_WIDTH
    gram_product = gram_product + ridge * jnp.eye(C, dtype=jnp.float32)
    cholesky_factor = jnp.linalg.cholesky(gram_product)
    return jnp.log(jnp.diagonal(cholesky_factor, axis1=1, axis2=2))

def reference(orbitals, w_first, w_second, pivots):
    sketch_first = jnp.dot(w_first.T.astype(jnp.float32), orbitals.astype(jnp.float32), preferred_element_type=jnp.float32)
    sketch_second = jnp.dot(w_second.T.astype(jnp.float32), orbitals.astype(jnp.float32), preferred_element_type=jnp.float32)
    pair_products = (sketch_first * sketch_second).astype(jnp.bfloat16)
    point_blocks = pair_products.reshape(SKETCH_WIDTH, N_GRID, 2 * C).transpose(1, 0, 2)
    chosen = jnp.take_along_axis(point_blocks, pivots[:, 0, None, :], axis=2)
    quality = log_pivots(chosen)
    positions = jnp.arange(N_GRID, dtype=jnp.int32)
    for section in range(1, ROUNDS):
        partner_bit = 1 << section - 1
        lower_set = chosen[positions - (positions & partner_bit)]
        upper_set = chosen[positions | partner_bit]
        merged = jnp.concatenate([lower_set, upper_set], axis=2)
        chosen = jnp.take_along_axis(merged, pivots[:, section, None, :], axis=2)
        quality = quality + log_pivots(chosen)
    return (chosen[0], quality)
```

```python
import jax
import jax.numpy as jnp
from jax import lax
from jax.experimental import pallas as pl
from jax.experimental.pallas import tpu as pltpu
from jax.sharding import PartitionSpec as P

MESH = pl.DeviceIdType.MESH
ridge = 0.1
NZ, NY, NX, NC = 16, 4, 4, 2
ROWS = 8
VM = pltpu.VMEM
DMA = pltpu.SemaphoreType.DMA


def place():
    g = lax.axis_index("grid")
    x = lax.axis_index("band")
    return x, g // 8, (g // 2) % 4, g % 2


def dev(x, z, y, c):
    return (z * 8 + y * 2 + c, x)


def barrier(peers):
    sem = pltpu.get_barrier_semaphore()
    for peer in peers:
        pl.semaphore_signal(sem, inc=1, device_id=peer, device_id_type=MESH)
    pl.semaphore_wait(sem, len(peers))


def send(src, dst, ssem, rsem, peer):
    copy = pltpu.make_async_remote_copy(src, dst, ssem, rsem, device_id=peer, device_id_type=MESH)
    copy.start()
    return copy


def drain(ref, sem):
    pltpu.make_async_copy(ref, ref, sem).wait()


def call(kernel, outs, scratch=(), cid=None, limit=None):
    single = not isinstance(outs, tuple)
    spec = pl.BlockSpec(memory_space=VM)
    params = {}
    if cid is not None:
        params.update(collective_id=cid, has_side_effects=True)
    if limit is not None:
        params.update(vmem_limit_bytes=limit)

    def run(*args):
        return pl.pallas_call(
            kernel,
            out_shape=outs,
            in_specs=[spec] * len(args),
            out_specs=spec if single else tuple(spec for _ in outs),
            scratch_shapes=list(scratch),
            compiler_params=pltpu.CompilerParams(**params),
        )(*args)

    return run


def shape(dims, dtype):
    return jax.ShapeDtypeStruct(dims, dtype)


Z_ORDER = (8, 7, 9, 6, 10, 5, 11, 4, 12, 3, 13, 2, 14, 1, 15)


def own_round(g):
    r = 1
    for bit in range(1, 7):
        r = r + jnp.where(g % (1 << bit) == 0, 1, 0)
    return r


def exchange_kernel(p_ref, wf_ref, ws_ref, ap_ref, wz_ref, pss, prs, qss, qrs, wss, wrs):
    x, z, y, c = place()
    yc = y * 2 + c
    barrier(
        [dev(x, lax.rem(z + d, 16), y, c) for d in range(1, 16)]
        + [dev(x, z, lax.rem(yc + d, 8) // 2, lax.rem(yc + d, 8) % 2) for d in range(1, 8)]
    )
    r = own_round(z * 8 + yc)
    ap_ref[z, yc, 0:1, :] = p_ref[0, 0:1, :]
    ap_ref[z, yc, 1:2, :] = p_ref[0, pl.ds(r, 1), :]
    mine = pl.multiple_of(z * 8, 8)
    wz_ref[pl.ds(mine, 8), 0:1024] = wf_ref[...]
    wz_ref[pl.ds(mine, 8), 1024:2048] = ws_ref[...]
    right, left = dev(x, lax.rem(z + 1, 16), y, c), dev(x, lax.rem(z + 15, 16), y, c)

    def hop(way, step):
        zz = lax.rem(z + 16 - step, 16) if way == 0 else lax.rem(z + step, 16)
        rows = pl.ds(pl.multiple_of(zz * 8, 8), 8)
        return send(
            wz_ref.at[rows], wz_ref.at[rows], wss.at[way, step], wrs.at[way, step], right if way == 0 else left
        )

    sends = []
    for d in Z_ORDER:
        send(ap_ref.at[z, yc], ap_ref.at[z, yc], pss, prs, dev(x, lax.rem(z + d, 16), y, c))
    for step in range(8):
        now = [hop(way, step) for way in (0, 1) if step < 7 or way == 0]
        sends += now
        if step == 2:
            drain(ap_ref.at[0:15, 0], prs)
            drain(ap_ref.at[0:15, 0], pss)
            for d in range(1, 8):
                o = lax.rem(yc + d, 8)
                send(ap_ref.at[:, yc], ap_ref.at[:, yc], qss, qrs, dev(x, z, o // 2, o % 2))
        for copy in now:
            copy.wait_recv()
    for copy in sends:
        copy.wait_send()
    drain(ap_ref.at[:, 0:7], qrs)
    drain(ap_ref.at[:, 0:7], qss)


def select_kernel(ap_ref, orb_ref, sel_ref, cand):
    def pick(parts, row):
        idx = jnp.broadcast_to(row, (8, 128))
        low, seg = idx & 127, idx >> 7
        out = jnp.take_along_axis(parts[0], low, axis=1)
        for s in range(1, 4):
            out = jnp.where(seg == s, jnp.take_along_axis(parts[s], low, axis=1), out)
        return out

    def first(k, _):
        cols = orb_ref[:, pl.ds(pl.multiple_of(k * 512, 512), 512)].astype(jnp.float32)
        parts = [cols[:, 128 * s : 128 * (s + 1)] for s in range(4)]
        t = (k // 8) * 16 + ((k // 2) % 4) * 4 + k % 2
        for h in range(2):
            got = pick(parts, ap_ref[k, 0:1, 128 * h : 128 * (h + 1)])
            cand[k, :, 128 * h : 128 * (h + 1)] = got
            sel_ref[t, :, 128 * h : 128 * (h + 1)] = got.astype(jnp.bfloat16)
        return 0

    sel_ref[2] = jnp.zeros((8, 256), jnp.bfloat16)
    lax.fori_loop(0, 128, first, 0, unroll=4)
    for r in range(1, 8):

        def later(k, _, r=r):
            lower, upper = cand[2 * k], cand[2 * k + 1]
            parts = [lower[:, :128], lower[:, 128:], upper[:, :128], upper[:, 128:]]
            o = k * (1 << r) + (1 << (r - 1))
            t = (o // 8) * 16 + ((o // 2) % 4) * 4 + 2 + o % 2
            got = [pick(parts, ap_ref[o, 1:2, 128 * h : 128 * (h + 1)]) for h in range(2)]
            for h in range(2):
                cand[k, :, 128 * h : 128 * (h + 1)] = got[h]
                sel_ref[t, :, 128 * h : 128 * (h + 1)] = got[h].astype(jnp.bfloat16)
            return 0

        count = 128 >> r
        lax.fori_loop(0, count, later, 0, unroll=min(4, count))


def spread_kernel(sel_ref, wz_ref, got_ref, w_ref, zss, zrs, ss, rs, lsem):
    x, z, y, c = place()
    xr, xl = dev(lax.rem(x + 1, 4), z, y, c), dev(lax.rem(x + 3, 4), z, y, c)
    yr, yl = dev(x, z, lax.rem(y + 1, 4), c), dev(x, z, lax.rem(y + 3, 4), c)
    barrier([dev(x, lax.rem(z + d, 16), y, c) for d in range(1, 16)] + [xr, xl, yr, yl])
    fc, sc = pl.ds(0, 1024), pl.ds(1024, 1024)
    waits = []

    def go(src, dst, i, peer):
        waits.append(send(src, dst, ss.at[i], rs.at[i], peer))
        return waits[-1]

    def unit(yy, xx, cols, rows=slice(None)):
        return w_ref.at[yy, xx, rows, cols]

    a0 = go(wz_ref.at[:, fc], unit(y, x, fc), 0, xr)
    a1 = go(wz_ref.at[:, fc], unit(y, x, fc), 1, xl)
    b0 = go(wz_ref.at[:, sc], unit(y, x, sc), 2, yr)
    b1 = go(wz_ref.at[:, sc], unit(y, x, sc), 3, yl)
    keep = pltpu.make_async_copy(wz_ref, w_ref.at[y, x], lsem.at[0])
    keep.start()
    for d in Z_ORDER:
        t = lax.rem(z + d, 16)
        send(sel_ref.at[t], got_ref.at[z], zss, zrs, dev(x, t, y, c))
    own = pltpu.make_async_copy(sel_ref.at[z], got_ref.at[z], lsem.at[1])
    own.start()
    lo, hi = pl.ds(0, 64), pl.ds(64, 64)
    xm, xp, ym, yp = lax.rem(x + 3, 4), lax.rem(x + 1, 4), lax.rem(y + 3, 4), lax.rem(y + 1, 4)
    a0.wait_recv()
    a2 = go(unit(y, xm, fc, lo), unit(y, xm, fc, lo), 4, xr)
    a1.wait_recv()
    a3 = go(unit(y, xp, fc, hi), unit(y, xp, fc, hi), 5, xl)
    b0.wait_recv()
    b2 = go(unit(ym, x, sc, lo), unit(ym, x, sc, lo), 6, yr)
    b1.wait_recv()
    b3 = go(unit(yp, x, sc, hi), unit(yp, x, sc, hi), 7, yl)
    keep.wait()
    a2.wait_recv()
    a3.wait_recv()
    every, low2, high2 = slice(None), slice(0, 2), slice(2, 4)

    def line(yy, part=every):
        return w_ref.at[yy, part, :, fc]

    def column(xx, part=every):
        return w_ref.at[part, xx, :, sc]

    a4 = go(line(y), line(y), 8, yr)
    a5 = go(line(y), line(y), 9, yl)
    b2.wait_recv()
    b3.wait_recv()
    b4 = go(column(x), column(x), 10, xr)
    b5 = go(column(x), column(x), 11, xl)
    a4.wait_recv()
    a6 = go(line(ym, low2), line(ym, low2), 12, yr)
    a5.wait_recv()
    a7 = go(line(yp, high2), line(yp, high2), 13, yl)
    b4.wait_recv()
    b6 = go(column(xm, low2), column(xm, low2), 14, xr)
    b5.wait_recv()
    b7 = go(column(xp, high2), column(xp, high2), 15, xl)
    for copy in (a6, a7, b6, b7):
        copy.wait_recv()
    for copy in waits:
        copy.wait_send()
    own.wait()
    drain(got_ref.at[0:15], zrs)
    drain(got_ref.at[0:15], zss)


def plane_kernel(r_ref, o_ref, ss, rs, lsem):
    x, z, y, c = place()
    p = y * 4 + x
    barrier([dev(lax.rem(p + d, 16) % 4, z, lax.rem(p + d, 16) // 4, c) for d in range(1, 16)])
    for d in range(1, 16):
        q = lax.rem(p + d, 16)
        send(r_ref.at[:, q], o_ref.at[p], ss, rs, dev(q % 4, z, q // 4, c))
    own = pltpu.make_async_copy(r_ref.at[:, p], o_ref.at[p], lsem)
    own.start()
    own.wait()
    drain(o_ref.at[0:15], rs)
    drain(o_ref.at[0:15], ss)


def sketch_kernel(o_ref, w_ref, s_ref):
    points = o_ref[...].T
    for n in range(0, 2048, 512):
        s_ref[:, n : n + 512] = jnp.dot(points, w_ref[:, n : n + 512], preferred_element_type=jnp.float32)


def swap_kernel(s_ref, o_ref, ss, rs):
    x, z, y, c = place()
    barrier([dev(x, z, y, 1 - c)])
    copy = send(s_ref, o_ref, ss, rs, dev(x, z, y, 1 - c))
    copy.wait()


def pivot_kernel(s_ref, o_ref, logs_ref, cols_ref, gram):
    total = s_ref[...] + o_ref[...]
    points = (total[:, :1024] * total[:, 1024:]).astype(jnp.bfloat16)
    product = lax.dot_general(points, points, (((1,), (1,)), ((), ())), preferred_element_type=jnp.float32)
    row = lax.broadcasted_iota(jnp.int32, (256, 256), 0)
    col = lax.broadcasted_iota(jnp.int32, (256, 256), 1)
    gram[...] = product / 1024 + jnp.where(row == col, ridge, 0.0)
    cols_ref[...] = points.T
    lane = lax.broadcasted_iota(jnp.int32, (8, 128), 1)
    sub = lax.broadcasted_iota(jnp.int32, (8, 128), 0)
    diag = [jnp.ones((8, 128), jnp.float32)] * 2
    for J in range(32):
        base = 8 * J
        halves = (0, 1) if J < 16 else (1,)
        h0 = base // 128
        panel = {h: gram[base : base + 8, 128 * h : 128 * h + 128] for h in halves}
        rows, inv = [], []
        for k in range(8):
            at = base + k - 128 * h0
            coef = jnp.broadcast_to(panel[h0][:, at : at + 1], (8, 128))
            pivot = jnp.broadcast_to(coef[k : k + 1, :], (8, 128))
            scale = 1.0 / pivot
            line = {h: jnp.broadcast_to(panel[h][k : k + 1, :], (8, 128)) for h in halves}
            diag[h0] = jnp.where(lane == at, pivot, diag[h0])
            rows.append({h: line[h] * scale for h in halves})
            factor = jnp.where(sub > k, coef, 0.0)
            panel = {h: panel[h] - factor * rows[k][h] for h in halves}

        def below(i, _, h0=h0, halves=halves, rows=rows, base=base):
            at0 = pl.ds(pl.multiple_of(i * 8, 8), 8)
            tile = {h: gram[at0, 128 * h : 128 * h + 128] for h in halves}
            for k in range(8):
                at = base + k - 128 * h0
                coef = jnp.broadcast_to(tile[h0][:, at : at + 1], (8, 128))
                tile = {h: tile[h] - coef * rows[k][h] for h in halves}
            for h in halves:
                gram[at0, 128 * h : 128 * h + 128] = tile[h]
            return 0

        left = 31 - J
        four = left // 4 * 4
        if four:
            lax.fori_loop(J + 1 + left - four, 32, below, 0, unroll=4)
        for i in range(J + 1, J + 1 + left - four):
            below(i, 0)
    logs_ref[:, 0:128] = 0.5 * jnp.log(diag[0][0:1, :])
    logs_ref[:, 128:256] = 0.5 * jnp.log(diag[1][0:1, :])


def finish_kernel(logs_ref, cols_ref, out_ref, q_ref, near, far, ns, nr, fs, fr, a_s, a_r, b_s, b_r, c_s, c_r, d_s, d_r, lsem):
    x, z, y, c = place()
    p = y * 4 + x
    plane = [dev(lax.rem(p + d, 16) % 4, z, lax.rem(p + d, 16) // 4, c) for d in range(1, 16)]
    deep = [dev(x, lax.rem(z + d, 16), y, c) for d in Z_ORDER]
    twin = dev(x, z, y, 1 - c)
    barrier(plane + deep + [twin])
    root_z, root_p = 8, 2
    is_root = jnp.logical_and(z == root_z, p == root_p)

    @pl.when(is_root)
    def _():
        for d in range(1, 16):
            q = lax.rem(p + d, 16)
            send(cols_ref.at[q, c], out_ref.at[q, c], a_s, a_r, dev(q % 4, z, q // 4, c))
        own = pltpu.make_async_copy(cols_ref.at[p, c], out_ref.at[p, c], lsem)
        own.start()
        own.wait()

    near[p] = logs_ref[...]
    for peer in plane:
        send(near.at[p], near.at[p], ns, nr, peer)

    @pl.when(jnp.logical_and(z == root_z, p != root_p))
    def _():
        drain(out_ref.at[0, 0], a_r)

    @pl.when(z == root_z)
    def _():
        for peer in deep:
            send(out_ref.at[p, c], out_ref.at[p, c], b_s, b_r, peer)

    drain(near.at[0:15], nr)
    drain(near.at[0:15], ns)
    far[z] = near[root_p]
    for peer in deep:
        send(far.at[z], far.at[z], fs, fr, peer)

    @pl.when(z != root_z)
    def _():
        drain(out_ref.at[0, 0], b_r)

    for peer in plane:
        send(out_ref.at[p, c], out_ref.at[p, c], c_s, c_r, peer)
    drain(far.at[0:15], fr)
    drain(far.at[0:15], fs)
    total = near[y * 4 + c]
    g = z * 8 + y * 2 + c
    for r in range(1, 8):
        k = g // (1 << r) * (1 << r) + (1 << (r - 1))
        if r < 4:
            o = k % 8
            total = total + near[(o // 2) * 4 + 2 + o % 2]
        else:
            total = total + far[k // 8]
    q_ref[...] = total
    drain(out_ref.at[0:15, 0], c_r)
    drain(out_ref.at[0:15, 0], c_s)
    last = send(out_ref.at[:, c], out_ref.at[:, c], d_s, d_r, twin)
    last.wait()

    @pl.when(is_root)
    def _():
        drain(out_ref.at[0:15, 0], a_s)

    @pl.when(z == root_z)
    def _():
        drain(out_ref.at[0:15, 0], b_s)


def local(orbitals, w_first, w_second, pivots):
    bf, f32 = jnp.bfloat16, jnp.float32
    lists, wz = call(
        exchange_kernel,
        (shape((16, 8, 2, 256), jnp.int32), shape((128, 2048), bf)),
        [DMA, DMA, DMA, DMA, DMA((2, 8)), DMA((2, 8))],
        cid=1,
    )(pivots, w_first, w_second)
    sel = call(select_kernel, shape((256, 8, 256), bf), [VM((128, 8, 256), f32)])(
        lists.reshape(128, 2, 256), orbitals
    )
    got, w = call(
        spread_kernel,
        (shape((16, 16, 8, 256), bf), shape((4, 4, 128, 2048), bf)),
        [DMA, DMA, DMA((16,)), DMA((16,)), DMA((2,))],
        cid=2,
    )(sel.reshape(16, 16, 8, 256), wz)
    points = call(plane_kernel, shape((16, 16, 8, 256), bf), [DMA, DMA, DMA], cid=3)(got)
    part = call(sketch_kernel, shape((256, 2048), f32))(points.reshape(2048, 256), w.reshape(2048, 2048))
    other = call(swap_kernel, shape((256, 2048), f32), [DMA, DMA], cid=4)(part)
    logs, cols = call(
        pivot_kernel, (shape((1, 256), f32), shape((1024, 256), bf)), [VM((256, 256), f32)]
    )(part, other)
    chosen, quality = call(
        finish_kernel,
        (shape((16, 2, 32, 256), bf), shape((1, 256), f32)),
        [VM((16, 1, 256), f32), VM((16, 1, 256), f32)] + [DMA] * 13,
        cid=5,
    )(logs, cols.reshape(16, 2, 32, 256))
    return chosen.reshape(1024, 256), quality


def solution(mesh):
    in_specs = (
        P(("band", "grid"), None),
        P(("band", "grid"), None),
        P(("band", "grid"), None),
        P("grid", None, None),
    )
    out_specs = (P(), P("grid", None))
    return jax.shard_map(local, mesh=mesh, in_specs=in_specs, out_specs=out_specs, check_vma=False)
```

```python
import jax
import jax.numpy as jnp
from jax import lax
from jax.experimental import pallas as pl
from jax.experimental.pallas import tpu as pltpu
from jax.sharding import PartitionSpec as P

MESH = pl.DeviceIdType.MESH
ridge = 0.1
NZ, NY, NX, NC = 16, 4, 4, 2
ROWS = 8
VM = pltpu.VMEM
DMA = pltpu.SemaphoreType.DMA


def place():
    g = lax.axis_index("grid")
    x = lax.axis_index("band")
    return x, g // 8, (g // 2) % 4, g % 2


def dev(x, z, y, c):
    return (z * 8 + y * 2 + c, x)


def barrier(peers):
    sem = pltpu.get_barrier_semaphore()
    for peer in peers:
        pl.semaphore_signal(sem, inc=1, device_id=peer, device_id_type=MESH)
    pl.semaphore_wait(sem, len(peers))


def send(src, dst, ssem, rsem, peer):
    copy = pltpu.make_async_remote_copy(src, dst, ssem, rsem, device_id=peer, device_id_type=MESH)
    copy.start()
    return copy


def drain(ref, sem):
    pltpu.make_async_copy(ref, ref, sem).wait()


def call(kernel, outs, scratch=(), cid=None, limit=None):
    single = not isinstance(outs, tuple)
    spec = pl.BlockSpec(memory_space=VM)
    params = {}
    if cid is not None:
        params.update(collective_id=cid, has_side_effects=True)
    if limit is not None:
        params.update(vmem_limit_bytes=limit)

    def run(*args):
        return pl.pallas_call(
            kernel,
            out_shape=outs,
            in_specs=[spec] * len(args),
            out_specs=spec if single else tuple(spec for _ in outs),
            scratch_shapes=list(scratch),
            compiler_params=pltpu.CompilerParams(**params),
        )(*args)

    return run


def shape(dims, dtype):
    return jax.ShapeDtypeStruct(dims, dtype)


Z_ORDER = (8, 7, 9, 6, 10, 5, 11, 4, 12, 3, 13, 2, 14, 1, 15)


def own_round(g):
    r = 1
    for bit in range(1, 7):
        r = r + jnp.where(g % (1 << bit) == 0, 1, 0)
    return r


def exchange_kernel(p_ref, wf_ref, ws_ref, ap_ref, wz_ref, pss, prs, qss, qrs, wss, wrs):
    x, z, y, c = place()
    yc = y * 2 + c
    barrier(
        [dev(x, lax.rem(z + d, 16), y, c) for d in range(1, 16)]
        + [dev(x, z, lax.rem(yc + d, 8) // 2, lax.rem(yc + d, 8) % 2) for d in range(1, 8)]
    )
    r = own_round(z * 8 + yc)
    ap_ref[z, yc, 0:1, :] = p_ref[0, 0:1, :]
    ap_ref[z, yc, 1:2, :] = p_ref[0, pl.ds(r, 1), :]
    mine = pl.multiple_of(z * 8, 8)
    wz_ref[pl.ds(mine, 8), 0:1024] = wf_ref[...]
    wz_ref[pl.ds(mine, 8), 1024:2048] = ws_ref[...]
    right, left = dev(x, lax.rem(z + 1, 16), y, c), dev(x, lax.rem(z + 15, 16), y, c)

    def hop(way, step):
        zz = lax.rem(z + 16 - step, 16) if way == 0 else lax.rem(z + step, 16)
        rows = pl.ds(pl.multiple_of(zz * 8, 8), 8)
        return send(
            wz_ref.at[rows], wz_ref.at[rows], wss.at[way, step], wrs.at[way, step], right if way == 0 else left
        )

    sends = []
    for d in Z_ORDER:
        send(ap_ref.at[z, yc], ap_ref.at[z, yc], pss, prs, dev(x, lax.rem(z + d, 16), y, c))
    for step in range(8):
        now = [hop(way, step) for way in (0, 1) if step < 7 or way == 0]
        sends += now
        if step == 2:
            drain(ap_ref.at[0:15, 0], prs)
            drain(ap_ref.at[0:15, 0], pss)
            for d in range(1, 8):
                o = lax.rem(yc + d, 8)
                send(ap_ref.at[:, yc], ap_ref.at[:, yc], qss, qrs, dev(x, z, o // 2, o % 2))
        for copy in now:
            copy.wait_recv()
    for copy in sends:
        copy.wait_send()
    drain(ap_ref.at[:, 0:7], qrs)
    drain(ap_ref.at[:, 0:7], qss)


def select_kernel(ap_ref, orb_ref, sel_ref, cand):
    def pick(parts, row):
        idx = jnp.broadcast_to(row, (8, 128))
        low, seg = idx & 127, idx >> 7
        out = jnp.take_along_axis(parts[0], low, axis=1)
        for s in range(1, 4):
            out = jnp.where(seg == s, jnp.take_along_axis(parts[s], low, axis=1), out)
        return out

    def first(k, _):
        cols = orb_ref[:, pl.ds(pl.multiple_of(k * 512, 512), 512)].astype(jnp.float32)
        parts = [cols[:, 128 * s : 128 * (s + 1)] for s in range(4)]
        t = (k // 8) * 16 + ((k // 2) % 4) * 4 + k % 2
        for h in range(2):
            got = pick(parts, ap_ref[k, 0:1, 128 * h : 128 * (h + 1)])
            cand[k, :, 128 * h : 128 * (h + 1)] = got
            sel_ref[t, :, 128 * h : 128 * (h + 1)] = got.astype(jnp.bfloat16)
        return 0

    sel_ref[2] = jnp.zeros((8, 256), jnp.bfloat16)
    lax.fori_loop(0, 128, first, 0, unroll=4)
    for r in range(1, 8):

        def later(k, _, r=r):
            lower, upper = cand[2 * k], cand[2 * k + 1]
            parts = [lower[:, :128], lower[:, 128:], upper[:, :128], upper[:, 128:]]
            o = k * (1 << r) + (1 << (r - 1))
            t = (o // 8) * 16 + ((o // 2) % 4) * 4 + 2 + o % 2
            got = [pick(parts, ap_ref[o, 1:2, 128 * h : 128 * (h + 1)]) for h in range(2)]
            for h in range(2):
                cand[k, :, 128 * h : 128 * (h + 1)] = got[h]
                sel_ref[t, :, 128 * h : 128 * (h + 1)] = got[h].astype(jnp.bfloat16)
            return 0

        count = 128 >> r
        lax.fori_loop(0, count, later, 0, unroll=min(4, count))


def spread_kernel(sel_ref, wz_ref, got_ref, w_ref, zss, zrs, ss, rs, lsem):
    x, z, y, c = place()
    xr, xl = dev(lax.rem(x + 1, 4), z, y, c), dev(lax.rem(x + 3, 4), z, y, c)
    yr, yl = dev(x, z, lax.rem(y + 1, 4), c), dev(x, z, lax.rem(y + 3, 4), c)
    barrier([dev(x, lax.rem(z + d, 16), y, c) for d in range(1, 16)] + [xr, xl, yr, yl])
    fc, sc = pl.ds(0, 1024), pl.ds(1024, 1024)
    waits = []

    def go(src, dst, i, peer):
        waits.append(send(src, dst, ss.at[i], rs.at[i], peer))
        return waits[-1]

    def unit(yy, xx, cols, rows=slice(None)):
        return w_ref.at[yy, xx, rows, cols]

    a0 = go(wz_ref.at[:, fc], unit(y, x, fc), 0, xr)
    a1 = go(wz_ref.at[:, fc], unit(y, x, fc), 1, xl)
    b0 = go(wz_ref.at[:, sc], unit(y, x, sc), 2, yr)
    b1 = go(wz_ref.at[:, sc], unit(y, x, sc), 3, yl)
    keep = pltpu.make_async_copy(wz_ref, w_ref.at[y, x], lsem.at[0])
    keep.start()
    for d in Z_ORDER:
        t = lax.rem(z + d, 16)
        send(sel_ref.at[t], got_ref.at[z], zss, zrs, dev(x, t, y, c))
    own = pltpu.make_async_copy(sel_ref.at[z], got_ref.at[z], lsem.at[1])
    own.start()
    lo, hi = pl.ds(0, 64), pl.ds(64, 64)
    xm, xp, ym, yp = lax.rem(x + 3, 4), lax.rem(x + 1, 4), lax.rem(y + 3, 4), lax.rem(y + 1, 4)
    a0.wait_recv()
    a2 = go(unit(y, xm, fc, lo), unit(y, xm, fc, lo), 4, xr)
    a1.wait_recv()
    a3 = go(unit(y, xp, fc, hi), unit(y, xp, fc, hi), 5, xl)
    b0.wait_recv()
    b2 = go(unit(ym, x, sc, lo), unit(ym, x, sc, lo), 6, yr)
    b1.wait_recv()
    b3 = go(unit(yp, x, sc, hi), unit(yp, x, sc, hi), 7, yl)
    keep.wait()
    a2.wait_recv()
    a3.wait_recv()
    every, low2, high2 = slice(None), slice(0, 2), slice(2, 4)

    def line(yy, part=every):
        return w_ref.at[yy, part, :, fc]

    def column(xx, part=every):
        return w_ref.at[part, xx, :, sc]

    a4 = go(line(y), line(y), 8, yr)
    a5 = go(line(y), line(y), 9, yl)
    b2.wait_recv()
    b3.wait_recv()
    b4 = go(column(x), column(x), 10, xr)
    b5 = go(column(x), column(x), 11, xl)
    a4.wait_recv()
    a6 = go(line(ym, low2), line(ym, low2), 12, yr)
    a5.wait_recv()
    a7 = go(line(yp, high2), line(yp, high2), 13, yl)
    b4.wait_recv()
    b6 = go(column(xm, low2), column(xm, low2), 14, xr)
    b5.wait_recv()
    b7 = go(column(xp, high2), column(xp, high2), 15, xl)
    for copy in (a6, a7, b6, b7):
        copy.wait_recv()
    for copy in waits:
        copy.wait_send()
    own.wait()
    drain(got_ref.at[0:15], zrs)
    drain(got_ref.at[0:15], zss)


def plane_kernel(r_ref, o_ref, ss, rs, lsem):
    x, z, y, c = place()
    p = y * 4 + x
    barrier([dev(lax.rem(p + d, 16) % 4, z, lax.rem(p + d, 16) // 4, c) for d in range(1, 16)])
    for d in range(1, 16):
        q = lax.rem(p + d, 16)
        send(r_ref.at[:, q], o_ref.at[p], ss, rs, dev(q % 4, z, q // 4, c))
    own = pltpu.make_async_copy(r_ref.at[:, p], o_ref.at[p], lsem)
    own.start()
    own.wait()
    drain(o_ref.at[0:15], rs)
    drain(o_ref.at[0:15], ss)


def sketch_kernel(o_ref, w_ref, s_ref):
    points = o_ref[...].T
    for n in range(0, 2048, 512):
        s_ref[:, n : n + 512] = jnp.dot(points, w_ref[:, n : n + 512], preferred_element_type=jnp.float32)


def swap_kernel(s_ref, o_ref, ss, rs):
    x, z, y, c = place()
    barrier([dev(x, z, y, 1 - c)])
    copy = send(s_ref, o_ref, ss, rs, dev(x, z, y, 1 - c))
    copy.wait()


def splat(row, at):
    return jnp.broadcast_to(row[:, at:at+1], (8,128))


def eliminate(gram, scaled, logs_ref, block=128):
    lane = lax.broadcasted_iota(jnp.int32, (8, 128), 1)
    diag = [jnp.ones((8, 128), jnp.float32)] * 2
    group = block // 8
    for J in range(32):
        base = 8 * J
        halves = (0, 1) if J < 16 else (1,)
        h0 = base // 128
        off = base - 128 * h0
        tile = {h: gram[base:base+8, 128*h:128*h+128] for h in halves}
        R = [{h: jnp.broadcast_to(tile[h][k:k+1, :], (8,128)) for h in halves} for k in range(8)]
        e = {(i, j): splat(R[i][h0], off + j) for i in range(8) for j in range(i, 8)}
        inv = []
        m = {}
        for k in range(8):
            inv.append(1.0 / e[k, k])
            for i in range(k+1, 8):
                m[i, k] = e[k, i] * inv[k]
            for i in range(k+1, 8):
                for j in range(i, 8):
                    e[i, j] = e[i, j] - m[i, k] * e[k, j]
                R[i] = {h: R[i][h] - m[i, k] * R[k][h] for h in halves}
            diag[h0] = jnp.where(lane == off + k, e[k, k], diag[h0])
        X = [{h: R[k][h] * inv[k] for h in halves} for k in range(8)]
        sub = lax.broadcasted_iota(jnp.int32, (8, 128), 0)
        for h in halves:
            u, s = R[0][h], X[0][h]
            for k in range(1, 8):
                u = jnp.where(sub == k, R[k][h], u)
                s = jnp.where(sub == k, X[k][h], s)
            gram[base:base+8, 128*h:128*h+128] = u
            scaled[base:base+8, 128*h:128*h+128] = s
        last = (J // group + 1) * group
        for i in range(J+1, last):
            t = {h: gram[8*i:8*i+8, 128*h:128*h+128] for h in halves}
            C = [splat(t[h0], off + k) for k in range(8)]
            for k in range(8):
                for q in range(k+1, 8):
                    C[q] = C[q] - C[k] * m[q, k]
            for h in halves:
                acc = t[h]
                for k in range(8):
                    acc = acc - C[k] * X[k][h]
                gram[8*i:8*i+8, 128*h:128*h+128] = acc
        if J % group == group-1 and J < 31:
            r0 = base + 8; p0 = r0 - block; c0 = r0 // 128 * 128
            upd = lax.dot_general(gram[p0:r0, r0//128*128:], scaled[p0:r0, c0:], (((0,),(0,)),((),())), precision=lax.Precision.HIGHEST, preferred_element_type=jnp.float32)
            cut = r0 - r0//128*128
            gram[r0:, c0:] = gram[r0:, c0:] - upd[cut:]
    logs_ref[:, 0:128] = 0.5 * jnp.log(diag[0][0:1, :])
    logs_ref[:, 128:256] = 0.5 * jnp.log(diag[1][0:1, :])


def pivot_kernel(s_ref, o_ref, logs_ref, cols_ref, gram, scaled):
    total = s_ref[...] + o_ref[...]
    points = (total[:, :1024] * total[:, 1024:]).astype(jnp.bfloat16)
    product = lax.dot_general(points, points, (((1,), (1,)), ((), ())), preferred_element_type=jnp.float32)
    row = lax.broadcasted_iota(jnp.int32, (256, 256), 0)
    col = lax.broadcasted_iota(jnp.int32, (256, 256), 1)
    gram[...] = product / 1024 + jnp.where(row == col, ridge, 0.0)
    cols_ref[...] = points.T
    eliminate(gram, scaled, logs_ref)


def finish_kernel(logs_ref, cols_ref, out_ref, q_ref, near, far, ns, nr, fs, fr, a_s, a_r, b_s, b_r, c_s, c_r, d_s, d_r, lsem):
    x, z, y, c = place()
    p = y * 4 + x
    plane = [dev(lax.rem(p + d, 16) % 4, z, lax.rem(p + d, 16) // 4, c) for d in range(1, 16)]
    deep = [dev(x, lax.rem(z + d, 16), y, c) for d in Z_ORDER]
    twin = dev(x, z, y, 1 - c)
    barrier(plane + deep + [twin])
    root_z, root_p = 8, 2
    is_root = jnp.logical_and(z == root_z, p == root_p)

    @pl.when(is_root)
    def _():
        for d in range(1, 16):
            q = lax.rem(p + d, 16)
            send(cols_ref.at[q, c], out_ref.at[q, c], a_s, a_r, dev(q % 4, z, q // 4, c))
        own = pltpu.make_async_copy(cols_ref.at[p, c], out_ref.at[p, c], lsem)
        own.start()
        own.wait()

    near[p] = logs_ref[...]
    for peer in plane:
        send(near.at[p], near.at[p], ns, nr, peer)

    @pl.when(jnp.logical_and(z == root_z, p != root_p))
    def _():
        drain(out_ref.at[0, 0], a_r)

    @pl.when(z == root_z)
    def _():
        for peer in deep:
            send(out_ref.at[p, c], out_ref.at[p, c], b_s, b_r, peer)

    drain(near.at[0:15], nr)
    drain(near.at[0:15], ns)
    far[z] = near[root_p]
    for peer in deep:
        send(far.at[z], far.at[z], fs, fr, peer)

    @pl.when(z != root_z)
    def _():
        drain(out_ref.at[0, 0], b_r)

    for peer in plane:
        send(out_ref.at[p, c], out_ref.at[p, c], c_s, c_r, peer)
    drain(far.at[0:15], fr)
    drain(far.at[0:15], fs)
    total = near[y * 4 + c]
    g = z * 8 + y * 2 + c
    for r in range(1, 8):
        k = g // (1 << r) * (1 << r) + (1 << (r - 1))
        if r < 4:
            o = k % 8
            total = total + near[(o // 2) * 4 + 2 + o % 2]
        else:
            total = total + far[k // 8]
    q_ref[...] = total
    drain(out_ref.at[0:15, 0], c_r)
    drain(out_ref.at[0:15, 0], c_s)
    last = send(out_ref.at[:, c], out_ref.at[:, c], d_s, d_r, twin)
    last.wait()

    @pl.when(is_root)
    def _():
        drain(out_ref.at[0:15, 0], a_s)

    @pl.when(z == root_z)
    def _():
        drain(out_ref.at[0:15, 0], b_s)


def local(orbitals, w_first, w_second, pivots):
    bf, f32 = jnp.bfloat16, jnp.float32
    lists, wz = call(
        exchange_kernel,
        (shape((16, 8, 2, 256), jnp.int32), shape((128, 2048), bf)),
        [DMA, DMA, DMA, DMA, DMA((2, 8)), DMA((2, 8))],
        cid=1,
    )(pivots, w_first, w_second)
    sel = call(select_kernel, shape((256, 8, 256), bf), [VM((128, 8, 256), f32)])(
        lists.reshape(128, 2, 256), orbitals
    )
    got, w = call(
        spread_kernel,
        (shape((16, 16, 8, 256), bf), shape((4, 4, 128, 2048), bf)),
        [DMA, DMA, DMA((16,)), DMA((16,)), DMA((2,))],
        cid=2,
    )(sel.reshape(16, 16, 8, 256), wz)
    points = call(plane_kernel, shape((16, 16, 8, 256), bf), [DMA, DMA, DMA], cid=3)(got)
    part = call(sketch_kernel, shape((256, 2048), f32))(points.reshape(2048, 256), w.reshape(2048, 2048))
    other = call(swap_kernel, shape((256, 2048), f32), [DMA, DMA], cid=4)(part)
    logs, cols = call(
        pivot_kernel, (shape((1, 256), f32), shape((1024, 256), bf)), [VM((256, 256), f32)] * 2
    )(part, other)
    chosen, quality = call(
        finish_kernel,
        (shape((16, 2, 32, 256), bf), shape((1, 256), f32)),
        [VM((16, 1, 256), f32), VM((16, 1, 256), f32)] + [DMA] * 13,
        cid=5,
    )(logs, cols.reshape(16, 2, 32, 256))
    return chosen.reshape(1024, 256), quality


def solution(mesh):
    in_specs = (
        P(("band", "grid"), None),
        P(("band", "grid"), None),
        P(("band", "grid"), None),
        P("grid", None, None),
    )
    out_specs = (P(), P("grid", None))
    return jax.shard_map(local, mesh=mesh, in_specs=in_specs, out_specs=out_specs, check_vma=False)
```

```python
import jax
import jax.numpy as jnp
from jax import lax
from jax.experimental import pallas as pl
from jax.experimental.pallas import tpu as pltpu
from jax.sharding import PartitionSpec as P

MESH = pl.DeviceIdType.MESH
ridge = 0.1
NZ, NY, NX, NC = 16, 4, 4, 2
ROWS = 8
VM = pltpu.VMEM
DMA = pltpu.SemaphoreType.DMA


def place():
    g = lax.axis_index("grid")
    x = lax.axis_index("band")
    return x, g // 8, (g // 2) % 4, g % 2


def dev(x, z, y, c):
    return (z * 8 + y * 2 + c, x)


def barrier(peers):
    sem = pltpu.get_barrier_semaphore()
    for peer in peers:
        pl.semaphore_signal(sem, inc=1, device_id=peer, device_id_type=MESH)
    pl.semaphore_wait(sem, len(peers))


def send(src, dst, ssem, rsem, peer):
    copy = pltpu.make_async_remote_copy(src, dst, ssem, rsem, device_id=peer, device_id_type=MESH)
    copy.start()
    return copy


def drain(ref, sem):
    pltpu.make_async_copy(ref, ref, sem).wait()


def call(kernel, outs, scratch=(), cid=None, limit=None, space=VM):
    single = not isinstance(outs, tuple)
    spec = pl.BlockSpec(memory_space=VM)
    params = {}
    if cid is not None:
        params.update(collective_id=cid, has_side_effects=True)
    if limit is not None:
        params.update(vmem_limit_bytes=limit)

    def run(*args):
        return pl.pallas_call(
            kernel,
            out_shape=outs,
            in_specs=[pl.BlockSpec(memory_space=space)] * len(args),
            out_specs=spec if single else tuple(spec for _ in outs),
            scratch_shapes=list(scratch),
            compiler_params=pltpu.CompilerParams(**params),
        )(*args)

    return run


def shape(dims, dtype):
    return jax.ShapeDtypeStruct(dims, dtype)


Z_ORDER = (8, 7, 9, 6, 10, 5, 11, 4, 12, 3, 13, 2, 14, 1, 15)


def own_round(g):
    r = 1
    for bit in range(1, 7):
        r = r + jnp.where(g % (1 << bit) == 0, 1, 0)
    return r


def splat(row, at):
    return jnp.broadcast_to(row[:, at:at+1], (8,128))


def eliminate(gram, scaled, logs_ref, hook, block=128):
    lane = lax.broadcasted_iota(jnp.int32, (8, 128), 1)
    diag = [jnp.ones((8, 128), jnp.float32)] * 2
    group = block // 8
    for J in range(32):
        base = 8 * J
        halves = (0, 1) if J < 16 else (1,)
        h0 = base // 128
        off = base - 128 * h0
        tile = {h: gram[base:base+8, 128*h:128*h+128] for h in halves}
        R = [{h: jnp.broadcast_to(tile[h][k:k+1, :], (8,128)) for h in halves} for k in range(8)]
        e = {(i, j): splat(R[i][h0], off + j) for i in range(8) for j in range(i, 8)}
        inv = []
        m = {}
        for k in range(8):
            inv.append(1.0 / e[k, k])
            for i in range(k+1, 8):
                m[i, k] = e[k, i] * inv[k]
            for i in range(k+1, 8):
                for j in range(i, 8):
                    e[i, j] = e[i, j] - m[i, k] * e[k, j]
                R[i] = {h: R[i][h] - m[i, k] * R[k][h] for h in halves}
            diag[h0] = jnp.where(lane == off + k, e[k, k], diag[h0])
        X = [{h: R[k][h] * inv[k] for h in halves} for k in range(8)]
        sub = lax.broadcasted_iota(jnp.int32, (8, 128), 0)
        for h in halves:
            u, s = R[0][h], X[0][h]
            for k in range(1, 8):
                u = jnp.where(sub == k, R[k][h], u)
                s = jnp.where(sub == k, X[k][h], s)
            gram[base:base+8, 128*h:128*h+128] = u
            scaled[base:base+8, 128*h:128*h+128] = s
        last = (J // group + 1) * group
        for i in range(J+1, last):
            t = {h: gram[8*i:8*i+8, 128*h:128*h+128] for h in halves}
            C = [splat(t[h0], off + k) for k in range(8)]
            for k in range(8):
                for q in range(k+1, 8):
                    C[q] = C[q] - C[k] * m[q, k]
            for h in halves:
                acc = t[h]
                for k in range(8):
                    acc = acc - C[k] * X[k][h]
                gram[8*i:8*i+8, 128*h:128*h+128] = acc
        if J % group == group-1 and J < 31:
            r0 = base + 8; p0 = r0 - block; c0 = r0 // 128 * 128
            upd = lax.dot_general(gram[p0:r0, r0//128*128:], scaled[p0:r0, c0:], (((0,),(0,)),((),())), precision=lax.Precision.HIGHEST, preferred_element_type=jnp.float32)
            cut = r0 - r0//128*128
            gram[r0:, c0:] = gram[r0:, c0:] - upd[cut:]
        hook(J)
    logs_ref[:, 0:128] = 0.5 * jnp.log(diag[0][0:1, :])
    logs_ref[:, 128:256] = 0.5 * jnp.log(diag[1][0:1, :])


def front_kernel(
    p_ref, wf_ref, ws_ref, orb_hbm, out_ref, q_ref,
    pv, orb_ref, cols, gram, scaled, near, far, ap, wz, w, cand, sel_a, sel_b, got_a, got_b, o, part, other,
    pss, prs, qss, qrs, wss, wrs, ss, rs, zas, zar, zbs, zbr, oas, oar, obs, obr, ts, tr, lsem, isem,
    ns, nr, fs, fr, a_s, a_r, b_s, b_r, c_s, c_r, d_s, d_r,
):
    x, z, y, c = place()
    p, yc = y * 4 + x, y * 2 + c
    twin = dev(x, z, y, 1 - c)
    xr, xl = dev(lax.rem(x + 1, 4), z, y, c), dev(lax.rem(x + 3, 4), z, y, c)
    yr, yl = dev(x, z, lax.rem(y + 1, 4), c), dev(x, z, lax.rem(y + 3, 4), c)

    def along(d):
        return dev(x, lax.rem(z + d, 16), y, c)

    mine = pl.multiple_of(z * 8, 8)
    loads = [
        pltpu.make_async_copy(p_ref, pv, isem.at[0]),
        pltpu.make_async_copy(wf_ref, wz.at[pl.ds(mine, 8), 0:1024], isem.at[1]),
        pltpu.make_async_copy(ws_ref, wz.at[pl.ds(mine, 8), 1024:2048], isem.at[2]),
        pltpu.make_async_copy(orb_hbm, orb_ref, isem.at[3]),
    ]
    for copy in loads:
        copy.start()
    loads[0].wait()
    r0 = own_round(z * 8 + yc)
    ap[z, yc, 0:1, :] = pv[0, 0:1, :]
    ap[z, yc, 1:2, :] = pv[0, pl.ds(r0, 1), :]
    barrier(
        [along(d) for d in range(1, 16)]
        + [dev(lax.rem(p + d, 16) % 4, z, lax.rem(p + d, 16) // 4, c) for d in range(1, 16)]
        + [dev(x, z, lax.rem(y + d, 4), 1 - c) for d in range(4)]
    )
    for d in Z_ORDER:
        send(ap.at[z, yc], ap.at[z, yc], pss, prs, along(d))
    waits = []
    arrive = {}

    def relay(stage):
        for way in (0, 1):
            if stage:
                arrive.pop((way, 2 * stage)).wait_recv()
            src = lax.rem(z + (16 - 2 * stage if way == 0 else 2 * stage), 16)
            rows = pl.ds(pl.multiple_of(src * 8, 8), 8)
            for step in (1, 2):
                far = 2 * stage + step
                if far == 8 and way == 1:
                    continue
                copy = send(
                    wz.at[rows], wz.at[rows], wss.at[way, far], wrs.at[way, far], along(step if way == 0 else 16 - step)
                )
                waits.append(copy)
                arrive[way, far] = copy

    loads[1].wait()
    loads[2].wait()
    relay(0)
    drain(ap.at[0:15, 0], prs)
    for d in range(1, 8):
        q = lax.rem(yc + d, 8)
        send(ap.at[:, yc], ap.at[:, yc], qss, qrs, dev(x, z, q // 2, q % 2))
    relay(1)
    drain(ap.at[:, 0:7], qrs)

    def pick(parts, row):
        idx = jnp.broadcast_to(row, (8, 128))
        low, seg = idx & 127, idx >> 7
        out = jnp.take_along_axis(parts[0], low, axis=1)
        for s in range(1, 4):
            out = jnp.where(seg == s, jnp.take_along_axis(parts[s], low, axis=1), out)
        return out

    def turn(i):
        return lax.rem(z + jnp.where(i % 2 == 1, 8 - (i + 1) // 2, 8 + i // 2), 16)

    def send_a(i):
        t = turn(i)
        send(sel_a.at[t], got_a.at[z], zas, zar, dev(x, t, y, c))

    def block(i, _):
        t = turn(i)

        def first(j, _):
            k = t * 8 + j
            cols = orb_ref[:, pl.ds(pl.multiple_of(k * 512, 512), 512)].astype(jnp.float32)
            parts = [cols[:, 128 * s : 128 * (s + 1)] for s in range(4)]
            for h in range(2):
                got = pick(parts, ap[t, j, 0:1, 128 * h : 128 * (h + 1)])
                cand[k, :, 128 * h : 128 * (h + 1)] = got
                sel_a[t, j, :, 128 * h : 128 * (h + 1)] = got.astype(jnp.bfloat16)
            return 0

        lax.fori_loop(0, 8, first, 0, unroll=4)

        @pl.when(i > 0)
        def _():
            send_a(i - 1)

        return 0

    loads[3].wait()
    lax.fori_loop(0, 3, block, 0)
    relay(2)
    lax.fori_loop(3, 6, block, 0)
    relay(3)
    lax.fori_loop(6, 10, block, 0)
    for copy in arrive.values():
        copy.wait_recv()
    fc, sc = pl.ds(0, 1024), pl.ds(1024, 1024)

    def go(src, dst, i, peer):
        waits.append(send(src, dst, ss.at[i], rs.at[i], peer))
        return waits[-1]

    def unit(yy, xx, cols, rows=slice(None)):
        return w.at[yy, xx, rows, cols]

    a0 = go(wz.at[:, fc], unit(y, x, fc), 0, xr)
    a1 = go(wz.at[:, fc], unit(y, x, fc), 1, xl)
    b0 = go(wz.at[:, sc], unit(y, x, sc), 2, yr)
    b1 = go(wz.at[:, sc], unit(y, x, sc), 3, yl)
    keep = pltpu.make_async_copy(wz, w.at[y, x], lsem.at[0])
    keep.start()
    lax.fori_loop(10, 16, block, 0)
    own_a = pltpu.make_async_copy(sel_a.at[z], got_a.at[z], lsem.at[1])
    own_a.start()
    lo, hi = pl.ds(0, 64), pl.ds(64, 64)
    xm, xp, ym, yp = lax.rem(x + 3, 4), lax.rem(x + 1, 4), lax.rem(y + 3, 4), lax.rem(y + 1, 4)
    a0.wait_recv()
    a2 = go(unit(y, xm, fc, lo), unit(y, xm, fc, lo), 4, xr)
    a1.wait_recv()
    a3 = go(unit(y, xp, fc, hi), unit(y, xp, fc, hi), 5, xl)
    b0.wait_recv()
    b2 = go(unit(ym, x, sc, lo), unit(ym, x, sc, lo), 6, yr)
    b1.wait_recv()
    b3 = go(unit(yp, x, sc, hi), unit(yp, x, sc, hi), 7, yl)

    sel_b[0, 0] = jnp.zeros((8, 256), jnp.bfloat16)
    for r in range(1, 8):

        def later(k, _, r=r):
            lower, upper = cand[2 * k], cand[2 * k + 1]
            parts = [lower[:, :128], lower[:, 128:], upper[:, :128], upper[:, 128:]]
            t = k * (1 << r) + (1 << (r - 1))
            got = [pick(parts, ap[t // 8, t % 8, 1:2, 128 * h : 128 * (h + 1)]) for h in range(2)]
            for h in range(2):
                cand[k, :, 128 * h : 128 * (h + 1)] = got[h]
                sel_b[t // 8, t % 8, :, 128 * h : 128 * (h + 1)] = got[h].astype(jnp.bfloat16)
            return 0

        count = 128 >> r
        lax.fori_loop(0, count, later, 0, unroll=min(4, count))

    keep.wait()
    a2.wait_recv()
    a3.wait_recv()
    every, low2, high2 = slice(None), slice(0, 2), slice(2, 4)

    def line(yy, part=every):
        return w.at[yy, part, :, fc]

    def column(xx, part=every):
        return w.at[part, xx, :, sc]

    a4 = go(line(y), line(y), 8, yr)
    a5 = go(line(y), line(y), 9, yl)
    b2.wait_recv()
    b3.wait_recv()
    b4 = go(column(x), column(x), 10, xr)
    b5 = go(column(x), column(x), 11, xl)
    for d in Z_ORDER:
        t = lax.rem(z + d, 16)
        send(sel_b.at[t], got_b.at[z], zbs, zbr, dev(x, t, y, c))
    own_b = pltpu.make_async_copy(sel_b.at[z], got_b.at[z], lsem.at[2])
    own_b.start()

    def hand(got, base, s_sem, r_sem, l_sem):
        for yy in range(4):
            for xx in range(2):
                src = got.at[:, yy * 2 + xx]
                same = jnp.logical_and(y == yy, x == base + xx)

                @pl.when(same)
                def _():
                    copy = pltpu.make_async_copy(src, o.at[p], l_sem)
                    copy.start()
                    copy.wait()

                @pl.when(jnp.logical_not(same))
                def _():
                    send(src, o.at[p], s_sem, r_sem, dev(base + xx, z, yy, c))

    own_a.wait()
    drain(got_a.at[0:15], zar)
    hand(got_a, 0, oas, oar, lsem.at[3])
    a4.wait_recv()
    a6 = go(line(ym, low2), line(ym, low2), 12, yr)
    a5.wait_recv()
    a7 = go(line(yp, high2), line(yp, high2), 13, yl)
    b4.wait_recv()
    b6 = go(column(xm, low2), column(xm, low2), 14, xr)
    b5.wait_recv()
    b7 = go(column(xp, high2), column(xp, high2), 15, xl)
    own_b.wait()
    drain(got_b.at[0:15], zbr)
    hand(got_b, 2, obs, obr, lsem.at[3])
    for copy in (a6, a7, b6, b7):
        copy.wait_recv()

    @pl.when(x < 2)
    def _():
        drain(o.at[0:15], oar)

    @pl.when(x >= 2)
    def _():
        drain(o.at[0:15], obr)

    points = o[...].reshape(2048, 256).T
    swaps = []
    for half in range(2):
        for n in range(0, 1024, 512):
            at = half * 1024 + n
            part[half, :, n : n + 512] = jnp.dot(
                points, w[:, :, :, at : at + 512].reshape(2048, 512), preferred_element_type=jnp.float32
            )
        swaps.append(send(part.at[half], other.at[half], ts.at[half], tr.at[half], twin))
    for copy in waits:
        copy.wait_send()
    drain(ap.at[0:15, 0], pss)
    drain(ap.at[:, 0:7], qss)
    drain(got_a.at[0:15], zas)
    drain(got_b.at[0:15], zbs)

    @pl.when(x < 2)
    def _():
        drain(o.at[0:7], oas)
        drain(o.at[0:8], obs)

    @pl.when(x >= 2)
    def _():
        drain(o.at[0:8], oas)
        drain(o.at[0:7], obs)

    for copy in swaps:
        copy.wait()
    chosen = ((part[0] + other[0]) * (part[1] + other[1])).astype(jnp.bfloat16)
    plane = [dev(lax.rem(p + d, 16) % 4, z, lax.rem(p + d, 16) // 4, c) for d in range(1, 16)]
    deep = [along(d) for d in Z_ORDER]
    root_z, root_p = 8, 2
    is_root = jnp.logical_and(z == root_z, p == root_p)

    @pl.when(is_root)
    def _():
        cols[...] = chosen.T.reshape(16, 2, 32, 256)
        for d in range(1, 16):
            q = lax.rem(p + d, 16)
            send(cols.at[q, c], out_ref.at[q, c], a_s, a_r, dev(q % 4, z, q // 4, c))
        own = pltpu.make_async_copy(cols.at[p, c], out_ref.at[p, c], lsem.at[3])
        own.start()
        own.wait()

    product = lax.dot_general(chosen, chosen, (((1,), (1,)), ((), ())), preferred_element_type=jnp.float32)
    row = lax.broadcasted_iota(jnp.int32, (256, 256), 0)
    col = lax.broadcasted_iota(jnp.int32, (256, 256), 1)
    gram[...] = product / 1024 + jnp.where(row == col, ridge, 0.0)

    def hook(done):
        if done != 11:
            return

        @pl.when(jnp.logical_and(z == root_z, p != root_p))
        def _():
            drain(out_ref.at[0, 0], a_r)

        @pl.when(z == root_z)
        def _():
            for peer in deep:
                send(out_ref.at[p, c], out_ref.at[p, c], b_s, b_r, peer)

    eliminate(gram, scaled, near.at[p], hook)
    for peer in plane:
        send(near.at[p], near.at[p], ns, nr, peer)

    @pl.when(z != root_z)
    def _():
        drain(out_ref.at[0, 0], b_r)

    for peer in plane:
        send(out_ref.at[p, c], out_ref.at[p, c], c_s, c_r, peer)
    drain(near.at[0:15], nr)
    drain(near.at[0:15], ns)
    far[z] = near[root_p]
    for peer in deep:
        send(far.at[z], far.at[z], fs, fr, peer)
    drain(out_ref.at[0:15, 0], c_r)
    drain(out_ref.at[0:15, 0], c_s)
    last = send(out_ref.at[:, c], out_ref.at[:, c], d_s, d_r, twin)
    drain(far.at[0:15], fr)
    drain(far.at[0:15], fs)
    total = near[y * 4 + c]
    g = z * 8 + yc
    for r in range(1, 8):
        k = g // (1 << r) * (1 << r) + (1 << (r - 1))
        if r < 4:
            j = k % 8
            total = total + near[(j // 2) * 4 + 2 + j % 2]
        else:
            total = total + far[k // 8]
    q_ref[...] = total
    last.wait()

    @pl.when(is_root)
    def _():
        drain(out_ref.at[0:15, 0], a_s)

    @pl.when(z == root_z)
    def _():
        drain(out_ref.at[0:15, 0], b_s)


def local(orbitals, w_first, w_second, pivots):
    bf, f32 = jnp.bfloat16, jnp.float32
    chosen, quality = call(
        front_kernel,
        (shape((16, 2, 32, 256), bf), shape((1, 256), f32)),
        [
            VM((1, 8, 256), jnp.int32),
            VM((8, 65536), bf),
            VM((16, 2, 32, 256), bf),
            VM((256, 256), f32),
            VM((256, 256), f32),
            VM((16, 1, 256), f32),
            VM((16, 1, 256), f32),
            VM((16, 8, 2, 256), jnp.int32),
            VM((128, 2048), bf),
            VM((4, 4, 128, 2048), bf),
            VM((128, 8, 256), f32),
            VM((16, 8, 8, 256), bf),
            VM((16, 8, 8, 256), bf),
            VM((16, 8, 8, 256), bf),
            VM((16, 8, 8, 256), bf),
            VM((16, 16, 8, 256), bf),
            VM((2, 256, 1024), f32),
            VM((2, 256, 1024), f32),
            DMA, DMA, DMA, DMA,
            DMA((2, 9)), DMA((2, 9)), DMA((16,)), DMA((16,)),
            DMA, DMA, DMA, DMA, DMA, DMA, DMA, DMA,
            DMA((2,)), DMA((2,)), DMA((4,)), DMA((4,)),
        ]
        + [DMA] * 12,
        cid=1,
        limit=67043328,
        space=pltpu.HBM,
    )(pivots, w_first, w_second, orbitals)
    return chosen.reshape(1024, 256), quality


def solution(mesh):
    in_specs = (
        P(("band", "grid"), None),
        P(("band", "grid"), None),
        P(("band", "grid"), None),
        P("grid", None, None),
    )
    out_specs = (P(), P("grid", None))
    return jax.shard_map(local, mesh=mesh, in_specs=in_specs, out_specs=out_specs, check_vma=False)
```
